32 devices in a mesh: elem: 8 (over z, y), dir: 4 (over x, core).
Axes of the slice: x: 2, y: 2, z: 4, core: 2. Of those that a mesh axis runs over, the one named last changes fastest.
Arguments:
- history: bfloat16 [8, 32, 3072], P(None, 'dir', 'elem'), may hold values from -6 to 6
- incident: bfloat16 [2, 32, 3072], P(None, 'dir', 'elem'), may hold values from -6 to 6
- ztiles: bfloat16 [24, 32, 128, 128], P('elem'), may hold values from -0.09375 to 0.09375
- zinv: bfloat16 [24, 128, 128], P('elem'), may hold values from -0.5 to 0.5
- columns: int32 [24, 32], P('elem'), may hold values from 0 to 23, as said below
- lags: int32 [24, 32], P('elem'), may hold values from 1 to 8
- counts: int32 [24], P('elem'), may hold values from 8 to 32
- basis: bfloat16 [3072, 256], P('elem'), may hold values from -0.15625 to 0.15625
Outputs:
- densities: bfloat16 [2, 32, 3072], P(None, 'dir', 'elem')
- far_field: float32 [2, 32, 256], P(None, 'dir', 'elem')
The draws below stay inside these ranges and needn't reach their ends.
Inputs may be any that keep to these rules, and one draw needn't show every extreme that they name: A block row's slots at or beyond counts are unused; a source block may repeat within a row. `columns`: all slots, used or not, of the block rows of one index of elem name blocks whose panels lie on any one index of elem at most 12 times, and exactly 12 times for some index.
All inputs are finite; a program needn't handle non-finite values.
Results may differ from the reference program's by a relative error of at most 0.005.
Values may be sent and summed in bfloat16 or wider, within the bound.
A program may use at most 64 MiB of HBM per device.

```python
import jax
import jax.numpy as jnp

PAN_DEV = 384
BLK = 128
K_MAX = 32
L = 8
DIRS = 32
SH = 256
STEPS = 2
PANELS = 3072
NBLK = 24
CAP = 12


def draw_columns(key, part):
    rows_dev = PAN_DEV // BLK
    devices_elem = NBLK // rows_dev
    slots_dev = rows_dev * K_MAX

    def one_device(dev_key):
        key_slots = jax.random.fold_in(dev_key, 11)
        key_owner = jax.random.fold_in(dev_key, 12)
        key_local = jax.random.fold_in(dev_key, 13)
        slot_order = jax.random.permutation(key_slots, slots_dev)
        owner_order = jax.random.permutation(key_owner, devices_elem)
        owner = owner_order[slot_order // CAP]
        local = jax.random.randint(key_local, (slots_dev,), 0, rows_dev)
        return (owner * rows_dev + local).astype(jnp.int32)
    dev_keys = jax.vmap(lambda index: jax.random.fold_in(key, index))(jnp.arange(devices_elem))
    blocks = jax.vmap(one_device)(dev_keys)
    return blocks.reshape(NBLK, K_MAX).astype(jnp.int32)


def set_ends(array, own_key, smallest, largest):
    spot = [jax.random.randint(jax.random.fold_in(own_key, axis), (), 0, length) for axis, length in enumerate(array.shape)]
    longest = array.shape.index(max(array.shape))
    beside = spot[:longest] + [(spot[longest] + 1) % array.shape[longest]] + spot[longest + 1:]
    return array.at[tuple(spot)].set(smallest).at[tuple(beside)].set(largest)


def strengthened(values, key, source, target, shards_of, factor):
    def block_of(axis_at):
        return (jnp.arange(values.shape[axis_at]) // (values.shape[axis_at] // shards_of)).reshape((-1,) + (1,) * (values.ndim - 1 - axis_at))

    first = jax.random.permutation(key, shards_of)[block_of(target)]
    second = (block_of(target) + shards_of // 2) % shards_of
    return jnp.where((block_of(source) == first) | (block_of(source) == second), factor * values, values)


def block_levels(own_key, shape, pieces, smallest, largest):
    def one(dim, parts):
        heights = jax.random.uniform(jax.random.fold_in(jax.random.fold_in(own_key, 6), dim), (parts,), jnp.float32, smallest / len(pieces), largest / len(pieces))
        return jnp.repeat(jnp.exp(heights), shape[dim] // parts).reshape((-1,) + (1,) * (len(shape) - dim - 1))

    loudness = one(*pieces[0])
    for cut in pieces[1:]:
        loudness = loudness * one(*cut)
    return loudness


def bell_draw(stream_key, shape, spread, most, pieces=(), held_as=jnp.bfloat16):
    drawn = jax.random.normal(stream_key, shape, jnp.float32) * spread
    if len(pieces) > 0:
        drawn = block_levels(stream_key, shape, pieces, -0.22, 0.18) * drawn
    return jnp.clip(drawn, min=-most, max=most).astype(held_as)


def bell_draw_with(rng, extent, scale, most, split, heavy, kind=jnp.bfloat16):
    result = scale * jax.random.normal(rng, extent, jnp.float32)
    if split:
        result = result * block_levels(rng, extent, split, -0.22, 0.18)
    return jnp.clip(strengthened(result, jax.random.fold_in(rng, 3), *heavy), -most, most).astype(kind)


def setup_inputs(seed: int = 0) -> dict:
    key_of = jax.random.split(jax.random.key(seed), 9)
    return {
        "history": bell_draw(key_of[0], (L, DIRS, PANELS), 1.0, 6.0, ((1, 4), (2, 8))),
        "incident": bell_draw(key_of[1], (STEPS, DIRS, PANELS), 1.0, 6.0, ((1, 4), (2, 8))),
        "ztiles": bell_draw(key_of[2], (NBLK, K_MAX, BLK, BLK), (BLK * K_MAX) ** -0.5, 0.09375, ((0, 8),)),
        "zinv": bell_draw(key_of[3], (NBLK, BLK, BLK), BLK ** -0.5, 0.5, ((0, 8),)),
        "columns": draw_columns(jax.random.fold_in(key_of[8], 71), 0),
        "lags": set_ends(jax.random.randint(key_of[5], (NBLK, K_MAX), 1, L + 1), jax.random.fold_in(key_of[5], 1), 1, L).astype(jnp.int32),
        "counts": set_ends(jax.random.randint(key_of[6], (NBLK,), max(1, K_MAX // 4), K_MAX + 1), jax.random.fold_in(key_of[6], 1), max(1, K_MAX // 4), K_MAX).astype(jnp.int32),
        "basis": bell_draw_with(key_of[7], (PANELS, SH), PANELS ** -0.5, 0.15625, ((0, 8),), (0, 1, 8, 2.0)),
    }


def reference(history, incident, ztiles, zinv, columns, lags, counts, basis):
    window = history
    slot_index = jnp.arange(K_MAX, dtype=jnp.int32)
    active = slot_index[None, :] < counts[:, None]
    dens_list = []
    far_list = []
    for step_index in range(STEPS):
        grid = window.reshape(L, DIRS, NBLK, BLK)
        picked = grid[lags - 1, :, columns, :]
        picked = jnp.where(active[:, :, None, None], picked, jnp.zeros((), picked.dtype))
        history_sum = jnp.einsum('rkdj,rkji->dri', picked.astype(jnp.float32), ztiles.astype(jnp.float32))
        own = incident[step_index].astype(jnp.float32).reshape(DIRS, NBLK, BLK)
        source = (own - history_sum).astype(jnp.bfloat16)
        density = jnp.einsum('drj,rji->dri', source.astype(jnp.float32), zinv.astype(jnp.float32))
        density = density.reshape(DIRS, PANELS).astype(jnp.bfloat16)
        far_part = jnp.dot(density, basis, preferred_element_type=jnp.float32)
        dens_list.append(density)
        far_list.append(far_part)
        window = jnp.concatenate([density[None], window[:-1]], axis=0)
    return jnp.stack(dens_list), jnp.stack(far_list)
```

```python
import functools

import jax
import jax.numpy as jnp
from jax import lax
from jax.experimental import pallas as pl
from jax.experimental.pallas import tpu as pltpu
from jax.sharding import PartitionSpec as P

MESH = pl.DeviceIdType.MESH
LANES = 128


def march_kernel(n, hist_hbm, inc_hbm, z_hbm, zinv_hbm, basis_hbm, where_from,
                 dens_out, far_out,
                 ext, ztile, zinv, basis, inc, picked, picked1, dens0, part, far_in,
                 load_sem, own_sem, hist_send, hist_recv, relay_send, dens_send, dens_recv,
                 far_send, far_recv):
    me = lax.axis_index("elem")
    _, rows, slots = where_from.shape
    levels, dirs, width = hist_hbm.shape
    half = n // 2
    partner = me + 1 - 2 * lax.rem(me, 2)
    owned = far_out.shape[2]

    per = levels * rows
    own_copies = [
        pltpu.make_async_copy(
            hist_hbm.at[level, :, pl.ds(row * LANES, LANES)],
            ext.at[me * per + level * rows + row], own_sem.at[level * rows + row])
        for level in range(levels) for row in range(rows)]
    for copy in own_copies:
        copy.start()
    loads = [
        pltpu.make_async_copy(z_hbm, ztile, load_sem.at[1]),
        pltpu.make_async_copy(zinv_hbm, zinv, load_sem.at[2]),
        pltpu.make_async_copy(basis_hbm, basis, load_sem.at[3]),
        pltpu.make_async_copy(inc_hbm, inc, load_sem.at[4]),
    ]
    barrier = pltpu.get_barrier_semaphore()
    for off in range(1, n):
        pl.semaphore_signal(barrier, inc=1, device_id={"elem": lax.rem(me + off, n)},
                            device_id_type=MESH)
    for load in loads:
        load.start()
    for copy in own_copies:
        copy.wait()
    pl.semaphore_wait(barrier, n - 1)

    def send_block(block, target, sem):
        return pltpu.make_async_remote_copy(
            src_ref=ext.at[pl.ds(block * per, per)],
            dst_ref=ext.at[pl.ds(block * per, per)],
            send_sem=sem, recv_sem=hist_recv.at[block],
            device_id={"elem": target}, device_id_type=MESH)

    sends = [send_block(me, partner, hist_send.at[0])]
    for off in range(1, half):
        sends.append(send_block(me, lax.rem(me + 2 * off, n), hist_send.at[off]))
    for copy in sends:
        copy.start()

    ext[n * per] = jnp.zeros((dirs, LANES), ext.dtype)
    dens0[n * rows] = jnp.zeros((dirs, LANES), dens0.dtype)

    relays = []
    for off in range(1, half):
        block = lax.rem(me + n - 2 * off, n)
        send_block(block, partner, relay_send.at[off]).wait_recv()
        relay = send_block(block, partner, relay_send.at[off])
        relay.start()
        relays.append(relay)
    send_block(partner, partner, relay_send.at[0]).wait_recv()
    for off in range(1, half):
        block = lax.rem(partner + n - 2 * off, n)
        send_block(block, partner, relay_send.at[off]).wait_recv()
    for copy in sends + relays:
        copy.wait_send()
    for load in loads:
        load.wait()

    sums = []
    for row in range(rows):
        for slot in range(slots):
            lanes = pl.ds(slot * LANES, LANES)
            picked[row, 0:dirs, lanes] = ext[where_from[0, row, slot]]
            picked[row, dirs:2 * dirs, lanes] = ext[where_from[1, row, slot]]
        sums.append(jnp.dot(picked[row], ztile[row], preferred_element_type=jnp.float32))

    def density_of(step, row, history_sum):
        own = inc[step, :, row * LANES:(row + 1) * LANES].astype(jnp.float32)
        source = (own - history_sum).astype(jnp.bfloat16)
        return jnp.dot(source, zinv[row], preferred_element_type=jnp.float32).astype(jnp.bfloat16)

    for row in range(rows):
        density = density_of(0, row, sums[row][0:dirs])
        dens0[me * rows + row] = density
        dens_out[0, :, row * LANES:(row + 1) * LANES] = density

    def send_density(off):
        return pltpu.make_async_remote_copy(
            src_ref=dens0.at[pl.ds(me * rows, rows)], dst_ref=dens0.at[pl.ds(me * rows, rows)],
            send_sem=dens_send.at[off], recv_sem=dens_recv.at[off],
            device_id={"elem": lax.rem(me + off, n)}, device_id_type=MESH)

    dens_copies = [send_density(off) for off in range(1, n)]
    for copy in dens_copies:
        copy.start()

    def far_copies(step):
        copies = []
        for off in range(1, n):
            target = lax.rem(me + off, n)
            tile = target * owned // LANES
            copies.append(pltpu.make_async_remote_copy(
                src_ref=part.at[step, tile], dst_ref=far_in.at[step, off],
                send_sem=far_send.at[step, off], recv_sem=far_recv.at[step, off],
                device_id={"elem": target}, device_id_type=MESH))
        return copies

    def far_parts(step, density):
        value = jnp.dot(density, basis[...], preferred_element_type=jnp.float32)
        for tile in range(part.shape[1]):
            part[step, tile] = value[:, tile * LANES:(tile + 1) * LANES]

    far_parts(0, dens_out[0])
    far0 = far_copies(0)
    for copy in far0:
        copy.start()

    for copy in dens_copies:
        copy.wait()
    for row in range(rows):
        for slot in range(slots):
            picked1[row, :, pl.ds(slot * LANES, LANES)] = dens0[where_from[2, row, slot]]
        total = sums[row][dirs:2 * dirs] + jnp.dot(
            picked1[row], ztile[row], preferred_element_type=jnp.float32)
        dens_out[1, :, row * LANES:(row + 1) * LANES] = density_of(1, row, total)
    far_parts(1, dens_out[1])
    far1 = far_copies(1)
    for copy in far1:
        copy.start()
    shift = lax.rem(me * owned, LANES)
    for step, copies in ((0, far0), (1, far1)):
        for copy in copies:
            copy.wait()
        total = part[step, me * owned // LANES]
        for off in range(1, n):
            total = total + far_in[step, off]
        total = pltpu.roll(total, lax.rem(LANES - shift, LANES), 1)
        far_out[step] = total[:, 0:owned]


def on_device(history, incident, ztiles, zinv, columns, lags, counts, basis, *, n):
    steps, dirs, width = incident.shape
    levels = history.shape[0]
    rows, slots, tile, _ = ztiles.shape
    coeffs = basis.shape[1]
    flat = ztiles.reshape(rows, slots * tile, tile)
    active = jnp.arange(slots, dtype=jnp.int32)[None, :] < counts[:, None]
    kind = jnp.arange(3, dtype=jnp.int32)[:, None, None]
    back = lags[None] - 1 - kind
    in_history = ((columns // rows)[None] * levels + back) * rows + (columns % rows)[None]
    where_from = jnp.where(
        kind < 2,
        jnp.where(active[None] & (back >= 0), in_history, n * levels * rows),
        jnp.where(active & (lags == 1), columns, n * rows)[None])
    any_spec = pl.BlockSpec(memory_space=pl.ANY)
    smem = pl.BlockSpec(memory_space=pltpu.SMEM)
    vmem = pl.BlockSpec(memory_space=pltpu.VMEM)
    bf16, f32 = jnp.bfloat16, jnp.float32
    dma = pltpu.SemaphoreType.DMA
    tiles = coeffs // LANES
    return pl.pallas_call(
        functools.partial(march_kernel, n),
        out_shape=(jax.ShapeDtypeStruct((steps, dirs, width), bf16),
                   jax.ShapeDtypeStruct((steps, dirs, coeffs // n), f32)),
        in_specs=[any_spec] * 5 + [smem],
        out_specs=(vmem, vmem),
        scratch_shapes=[
            pltpu.VMEM((n * levels * rows + 1, dirs, LANES), bf16),
            pltpu.VMEM(flat.shape, bf16),
            pltpu.VMEM(zinv.shape, bf16),
            pltpu.VMEM(basis.shape, bf16),
            pltpu.VMEM(incident.shape, bf16),
            pltpu.VMEM((rows, 2 * dirs, slots * tile), bf16),
            pltpu.VMEM((rows, dirs, slots * tile), bf16),
            pltpu.VMEM((n * rows + 1, dirs, LANES), bf16),
            pltpu.VMEM((steps, tiles, dirs, LANES), f32),
            pltpu.VMEM((steps, n, dirs, LANES), f32),
            dma((5,)), dma((levels * rows,)),
            dma((n,)), dma((n,)), dma((n,)),
            dma((n,)), dma((n,)),
            dma((steps, n)), dma((steps, n)),
        ],
        compiler_params=pltpu.CompilerParams(
            collective_id=0, has_side_effects=True, vmem_limit_bytes=48 * 1024 * 1024),
    )(history, incident, flat, zinv, basis, where_from)


def solution(mesh):
    in_specs = (
        P(None, "dir", "elem"),
        P(None, "dir", "elem"),
        P("elem", None, None, None),
        P("elem", None, None),
        P("elem", None),
        P("elem", None),
        P("elem"),
        P("elem", None),
    )
    out_specs = (P(None, "dir", "elem"), P(None, "dir", "elem"))
    return jax.shard_map(
        functools.partial(on_device, n=mesh.shape["elem"]), mesh=mesh,
        in_specs=in_specs, out_specs=out_specs, check_vma=False)
```

```python
import functools

import jax
import jax.numpy as jnp
from jax import lax
from jax.experimental import pallas as pl
from jax.experimental.pallas import tpu as pltpu
from jax.sharding import PartitionSpec as P

MESH = pl.DeviceIdType.MESH
LANES = 128


def march_kernel(n, hist_hbm, inc_hbm, z_hbm, zinv_hbm, basis_hbm, cols, lags, counts,
                 dens_out, far_out,
                 ext, ztile, zinv, basis, inc, picked, picked1, dens0, part, far_in,
                 load_sem, own_sem, hist_send, hist_recv, relay_send, dens_send, dens_recv,
                 far_send, far_recv):
    me = lax.axis_index("elem")
    rows, slots = cols.shape
    levels, dirs, width = hist_hbm.shape
    half = n // 2
    partner = me + 1 - 2 * lax.rem(me, 2)
    owned = far_out.shape[2]

    per = levels * rows
    own_copies = [
        pltpu.make_async_copy(
            hist_hbm.at[level, :, pl.ds(row * LANES, LANES)],
            ext.at[me * per + level * rows + row], own_sem.at[level * rows + row])
        for level in range(levels) for row in range(rows)]
    for copy in own_copies:
        copy.start()
    loads = [
        pltpu.make_async_copy(z_hbm, ztile, load_sem.at[1]),
        pltpu.make_async_copy(zinv_hbm, zinv, load_sem.at[2]),
        pltpu.make_async_copy(basis_hbm, basis, load_sem.at[3]),
        pltpu.make_async_copy(inc_hbm, inc, load_sem.at[4]),
    ]
    barrier = pltpu.get_barrier_semaphore()
    for off in range(1, n):
        pl.semaphore_signal(barrier, inc=1, device_id={"elem": lax.rem(me + off, n)},
                            device_id_type=MESH)
    for load in loads:
        load.start()
    for copy in own_copies:
        copy.wait()
    pl.semaphore_wait(barrier, n - 1)

    def send_block(block, target, sem):
        return pltpu.make_async_remote_copy(
            src_ref=ext.at[pl.ds(block * per, per)],
            dst_ref=ext.at[pl.ds(block * per, per)],
            send_sem=sem, recv_sem=hist_recv.at[block],
            device_id={"elem": target}, device_id_type=MESH)

    sends = [send_block(me, partner, hist_send.at[0])]
    for off in range(1, half):
        sends.append(send_block(me, lax.rem(me + 2 * off, n), hist_send.at[off]))
    for copy in sends:
        copy.start()

    ext[n * per] = jnp.zeros((dirs, LANES), ext.dtype)
    dens0[n * rows] = jnp.zeros((dirs, LANES), dens0.dtype)

    from_hist0, from_hist1, from_dens = [], [], []
    for row in range(rows):
        live = counts[row]
        for slot in range(slots):
            column, lag = cols[row, slot], lags[row, slot]
            lag = jnp.where(slot < live, lag, 0)
            base = lax.div(column, rows) * per + lax.rem(column, rows) - rows
            newest = base + lag * rows
            from_hist0.append(jnp.where(lag > 0, newest, n * per))
            from_hist1.append(jnp.where(lag > 1, newest - rows, n * per))
            from_dens.append(jnp.where(lag == 1, column, n * rows))

    relays = []
    for off in range(1, half):
        block = lax.rem(me + n - 2 * off, n)
        send_block(block, partner, relay_send.at[off]).wait_recv()
        relay = send_block(block, partner, relay_send.at[off])
        relay.start()
        relays.append(relay)
    send_block(partner, partner, relay_send.at[0]).wait_recv()
    for off in range(1, half):
        block = lax.rem(partner + n - 2 * off, n)
        send_block(block, partner, relay_send.at[off]).wait_recv()
    for copy in sends + relays:
        copy.wait_send()
    for load in loads:
        load.wait()

    sums = []
    for row in range(rows):
        for slot in range(slots):
            lanes = pl.ds(slot * LANES, LANES)
            picked[row, 0:dirs, lanes] = ext[from_hist0[row * slots + slot]]
            picked[row, dirs:2 * dirs, lanes] = ext[from_hist1[row * slots + slot]]
        sums.append(jnp.dot(picked[row], ztile[row], preferred_element_type=jnp.float32))

    def density_of(step, row, history_sum):
        own = inc[step, :, row * LANES:(row + 1) * LANES].astype(jnp.float32)
        source = (own - history_sum).astype(jnp.bfloat16)
        return jnp.dot(source, zinv[row], preferred_element_type=jnp.float32).astype(jnp.bfloat16)

    for row in range(rows):
        density = density_of(0, row, sums[row][0:dirs])
        dens0[me * rows + row] = density
        dens_out[0, :, row * LANES:(row + 1) * LANES] = density

    def send_density(off):
        return pltpu.make_async_remote_copy(
            src_ref=dens0.at[pl.ds(me * rows, rows)], dst_ref=dens0.at[pl.ds(me * rows, rows)],
            send_sem=dens_send.at[off], recv_sem=dens_recv.at[off],
            device_id={"elem": lax.rem(me + off, n)}, device_id_type=MESH)

    dens_copies = [send_density(off) for off in range(1, n)]
    for copy in dens_copies:
        copy.start()

    def far_copies(step):
        copies = []
        for off in range(1, n):
            target = lax.rem(me + off, n)
            tile = target * owned // LANES
            copies.append(pltpu.make_async_remote_copy(
                src_ref=part.at[step, tile], dst_ref=far_in.at[step, off],
                send_sem=far_send.at[step, off], recv_sem=far_recv.at[step, off],
                device_id={"elem": target}, device_id_type=MESH))
        return copies

    def far_parts(step, density):
        value = jnp.dot(density, basis[...], preferred_element_type=jnp.float32)
        for tile in range(part.shape[1]):
            part[step, tile] = value[:, tile * LANES:(tile + 1) * LANES]

    far_parts(0, dens_out[0])
    far0 = far_copies(0)
    for copy in far0:
        copy.start()

    for copy in dens_copies:
        copy.wait()
    for row in range(rows):
        for slot in range(slots):
            picked1[row, :, pl.ds(slot * LANES, LANES)] = dens0[from_dens[row * slots + slot]]
        total = sums[row][dirs:2 * dirs] + jnp.dot(
            picked1[row], ztile[row], preferred_element_type=jnp.float32)
        dens_out[1, :, row * LANES:(row + 1) * LANES] = density_of(1, row, total)
    far_parts(1, dens_out[1])
    far1 = far_copies(1)
    for copy in far1:
        copy.start()
    shift = lax.rem(me * owned, LANES)
    for step, copies in ((0, far0), (1, far1)):
        for copy in copies:
            copy.wait()
        total = part[step, me * owned // LANES]
        for off in range(1, n):
            total = total + far_in[step, off]
        total = pltpu.roll(total, lax.rem(LANES - shift, LANES), 1)
        far_out[step] = total[:, 0:owned]


def on_device(history, incident, ztiles, zinv, columns, lags, counts, basis, *, n):
    steps, dirs, width = incident.shape
    levels = history.shape[0]
    rows, slots, tile, _ = ztiles.shape
    coeffs = basis.shape[1]
    flat = ztiles.reshape(rows, slots * tile, tile)
    hbm = pl.BlockSpec(memory_space=pltpu.HBM)
    smem = pl.BlockSpec(memory_space=pltpu.SMEM)
    vmem = pl.BlockSpec(memory_space=pltpu.VMEM)
    bf16, f32 = jnp.bfloat16, jnp.float32
    dma = pltpu.SemaphoreType.DMA
    tiles = coeffs // LANES
    return pl.pallas_call(
        functools.partial(march_kernel, n),
        out_shape=(jax.ShapeDtypeStruct((steps, dirs, width), bf16),
                   jax.ShapeDtypeStruct((steps, dirs, coeffs // n), f32)),
        in_specs=[hbm] * 5 + [smem] * 3,
        out_specs=(vmem, vmem),
        scratch_shapes=[
            pltpu.VMEM((n * levels * rows + 1, dirs, LANES), bf16),
            pltpu.VMEM(flat.shape, bf16),
            pltpu.VMEM(zinv.shape, bf16),
            pltpu.VMEM(basis.shape, bf16),
            pltpu.VMEM(incident.shape, bf16),
            pltpu.VMEM((rows, 2 * dirs, slots * tile), bf16),
            pltpu.VMEM((rows, dirs, slots * tile), bf16),
            pltpu.VMEM((n * rows + 1, dirs, LANES), bf16),
            pltpu.VMEM((steps, tiles, dirs, LANES), f32),
            pltpu.VMEM((steps, n, dirs, LANES), f32),
            dma((5,)), dma((levels * rows,)),
            dma((n,)), dma((n,)), dma((n,)),
            dma((n,)), dma((n,)),
            dma((steps, n)), dma((steps, n)),
        ],
        compiler_params=pltpu.CompilerParams(
            collective_id=0, has_side_effects=True, vmem_limit_bytes=67043328),
    )(history, incident, flat, zinv, basis, columns, lags, counts)


def solution(mesh):
    in_specs = (
        P(None, "dir", "elem"),
        P(None, "dir", "elem"),
        P("elem", None, None, None),
        P("elem", None, None),
        P("elem", None),
        P("elem", None),
        P("elem"),
        P("elem", None),
    )
    out_specs = (P(None, "dir", "elem"), P(None, "dir", "elem"))
    return jax.shard_map(
        functools.partial(on_device, n=mesh.shape["elem"]), mesh=mesh,
        in_specs=in_specs, out_specs=out_specs, check_vma=False)
```

```python
import functools

import jax
import jax.numpy as jnp
from jax import lax
from jax.experimental import pallas as pl
from jax.experimental.pallas import tpu as pltpu
from jax.sharding import PartitionSpec as P

MESH = pl.DeviceIdType.MESH
LANES = 128


def march_kernel(n, hist_hbm, inc_hbm, z_hbm, zinv_hbm, basis_hbm, cols_hbm,
                 lags_hbm, counts_hbm,
                 dens_out, far_out,
                 ext, ztile, zinv, basis, inc, cols, lags, counts, picked, picked1, dens0, part, far_in,
                 load_sem, own_sem, hist_send, hist_recv, relay_send, dens_send, dens_recv,
                 far_send, far_recv):
    me = lax.axis_index("elem")
    rows, slots = cols.shape
    levels, dirs, width = hist_hbm.shape
    half = n // 2
    partner = me + 1 - 2 * lax.rem(me, 2)
    owned = far_out.shape[2]

    per = levels * rows
    own_copies = [
        pltpu.make_async_copy(
            hist_hbm.at[level, :, pl.ds(row * LANES, LANES)],
            ext.at[me * per + level * rows + row], own_sem.at[level * rows + row])
        for level in range(levels) for row in range(rows)]
    for copy in own_copies:
        copy.start()
    tables = [
        pltpu.make_async_copy(cols_hbm, cols, load_sem.at[0]),
        pltpu.make_async_copy(lags_hbm, lags, load_sem.at[5]),
        pltpu.make_async_copy(counts_hbm, counts, load_sem.at[6]),
    ]
    loads = [
        pltpu.make_async_copy(z_hbm, ztile, load_sem.at[1]),
        pltpu.make_async_copy(zinv_hbm, zinv, load_sem.at[2]),
        pltpu.make_async_copy(basis_hbm, basis, load_sem.at[3]),
        pltpu.make_async_copy(inc_hbm, inc, load_sem.at[4]),
    ]
    barrier = pltpu.get_barrier_semaphore()
    for off in range(1, n):
        pl.semaphore_signal(barrier, inc=1, device_id={"elem": lax.rem(me + off, n)},
                            device_id_type=MESH)
    for load in tables + loads:
        load.start()
    ext[n * per] = jnp.zeros((dirs, LANES), ext.dtype)
    dens0[n * rows] = jnp.zeros((dirs, LANES), dens0.dtype)

    for load in tables:
        load.wait()
    from_hist0, from_hist1, from_dens = [], [], []
    for row in range(rows):
        live = counts[row]
        for slot in range(slots):
            column, lag = cols[row, slot], lags[row, slot]
            lag = jnp.where(slot < live, lag, 0)
            base = lax.div(column, rows) * per + lax.rem(column, rows) - rows
            newest = base + lag * rows
            from_hist0.append(jnp.where(lag > 0, newest, n * per))
            from_hist1.append(jnp.where(lag > 1, newest - rows, n * per))
            from_dens.append(jnp.where(lag == 1, column, n * rows))

    for copy in own_copies:
        copy.wait()
    pl.semaphore_wait(barrier, n - 1)

    def send_block(block, target, sem):
        return pltpu.make_async_remote_copy(
            src_ref=ext.at[pl.ds(block * per, per)],
            dst_ref=ext.at[pl.ds(block * per, per)],
            send_sem=sem, recv_sem=hist_recv.at[block],
            device_id={"elem": target}, device_id_type=MESH)

    sends = [send_block(me, partner, hist_send.at[0])]
    for off in range(1, half):
        sends.append(send_block(me, lax.rem(me + 2 * off, n), hist_send.at[off]))
    for copy in sends:
        copy.start()

    relays = []
    for off in range(1, half):
        block = lax.rem(me + n - 2 * off, n)
        send_block(block, partner, relay_send.at[off]).wait_recv()
        relay = send_block(block, partner, relay_send.at[off])
        relay.start()
        relays.append(relay)
    send_block(partner, partner, relay_send.at[0]).wait_recv()
    for off in range(1, half):
        block = lax.rem(partner + n - 2 * off, n)
        send_block(block, partner, relay_send.at[off]).wait_recv()
    for copy in sends + relays:
        copy.wait_send()
    for load in loads:
        load.wait()

    sums = []
    for row in range(rows):
        for slot in range(slots):
            lanes = pl.ds(slot * LANES, LANES)
            picked[row, 0:dirs, lanes] = ext[from_hist0[row * slots + slot]]
            picked[row, dirs:2 * dirs, lanes] = ext[from_hist1[row * slots + slot]]
        sums.append(jnp.dot(picked[row], ztile[row], preferred_element_type=jnp.float32))

    def density_of(step, row, history_sum):
        own = inc[step, :, row * LANES:(row + 1) * LANES].astype(jnp.float32)
        source = (own - history_sum).astype(jnp.bfloat16)
        return jnp.dot(source, zinv[row], preferred_element_type=jnp.float32).astype(jnp.bfloat16)

    for row in range(rows):
        density = density_of(0, row, sums[row][0:dirs])
        dens0[me * rows + row] = density
        dens_out[0, :, row * LANES:(row + 1) * LANES] = density

    def send_density(off):
        return pltpu.make_async_remote_copy(
            src_ref=dens0.at[pl.ds(me * rows, rows)], dst_ref=dens0.at[pl.ds(me * rows, rows)],
            send_sem=dens_send.at[off], recv_sem=dens_recv.at[off],
            device_id={"elem": lax.rem(me + off, n)}, device_id_type=MESH)

    dens_copies = [send_density(off) for off in range(1, n)]
    for copy in dens_copies:
        copy.start()

    def far_copies(step):
        copies = []
        for off in range(1, n):
            target = lax.rem(me + off, n)
            tile = target * owned // LANES
            copies.append(pltpu.make_async_remote_copy(
                src_ref=part.at[step, tile], dst_ref=far_in.at[step, off],
                send_sem=far_send.at[step, off], recv_sem=far_recv.at[step, off],
                device_id={"elem": target}, device_id_type=MESH))
        return copies

    def far_parts(step, density):
        value = jnp.dot(density, basis[...], preferred_element_type=jnp.float32)
        for tile in range(part.shape[1]):
            part[step, tile] = value[:, tile * LANES:(tile + 1) * LANES]

    far_parts(0, dens_out[0])
    far0 = far_copies(0)
    for copy in far0:
        copy.start()

    for copy in dens_copies:
        copy.wait()
    for row in range(rows):
        for slot in range(slots):
            picked1[row, :, pl.ds(slot * LANES, LANES)] = dens0[from_dens[row * slots + slot]]
        total = sums[row][dirs:2 * dirs] + jnp.dot(
            picked1[row], ztile[row], preferred_element_type=jnp.float32)
        dens_out[1, :, row * LANES:(row + 1) * LANES] = density_of(1, row, total)
    far_parts(1, dens_out[1])
    far1 = far_copies(1)
    for copy in far1:
        copy.start()
    shift = lax.rem(me * owned, LANES)
    for step, copies in ((0, far0), (1, far1)):
        for copy in copies:
            copy.wait()
        total = part[step, me * owned // LANES]
        for off in range(1, n):
            total = total + far_in[step, off]
        total = pltpu.roll(total, lax.rem(LANES - shift, LANES), 1)
        far_out[step] = total[:, 0:owned]


def on_device(history, incident, ztiles, zinv, columns, lags, counts, basis, *, n):
    steps, dirs, width = incident.shape
    levels = history.shape[0]
    rows, slots, tile, _ = ztiles.shape
    coeffs = basis.shape[1]
    flat = ztiles.reshape(rows, slots * tile, tile)
    hbm = pl.BlockSpec(memory_space=pltpu.HBM)
    vmem = pl.BlockSpec(memory_space=pltpu.VMEM)
    bf16, f32 = jnp.bfloat16, jnp.float32
    dma = pltpu.SemaphoreType.DMA
    tiles = coeffs // LANES
    return pl.pallas_call(
        functools.partial(march_kernel, n),
        out_shape=(pltpu.VMEM((steps, dirs, width), bf16),
                   pltpu.VMEM((steps, dirs, coeffs // n), f32)),
        in_specs=[hbm] * 8,
        out_specs=(vmem, vmem),
        scratch_shapes=[
            pltpu.VMEM((n * levels * rows + 1, dirs, LANES), bf16),
            pltpu.VMEM(flat.shape, bf16),
            pltpu.VMEM(zinv.shape, bf16),
            pltpu.VMEM(basis.shape, bf16),
            pltpu.VMEM(incident.shape, bf16),
            pltpu.SMEM(columns.shape, jnp.int32),
            pltpu.SMEM(lags.shape, jnp.int32),
            pltpu.SMEM(counts.shape, jnp.int32),
            pltpu.VMEM((rows, 2 * dirs, slots * tile), bf16),
            pltpu.VMEM((rows, dirs, slots * tile), bf16),
            pltpu.VMEM((n * rows + 1, dirs, LANES), bf16),
            pltpu.VMEM((steps, tiles, dirs, LANES), f32),
            pltpu.VMEM((steps, n, dirs, LANES), f32),
            dma((7,)), dma((levels * rows,)),
            dma((n,)), dma((n,)), dma((n,)),
            dma((n,)), dma((n,)),
            dma((steps, n)), dma((steps, n)),
        ],
        compiler_params=pltpu.CompilerParams(
            collective_id=0, has_side_effects=True, vmem_limit_bytes=32 * 1024 * 1024),
    )(*(pltpu.with_memory_space_constraint(x, pltpu.HBM)
        for x in (history, incident, flat, zinv, basis, columns, lags, counts)))


def solution(mesh):
    in_specs = (
        P(None, "dir", "elem"),
        P(None, "dir", "elem"),
        P("elem", None, None, None),
        P("elem", None, None),
        P("elem", None),
        P("elem", None),
        P("elem"),
        P("elem", None),
    )
    out_specs = (P(None, "dir", "elem"), P(None, "dir", "elem"))
    return jax.shard_map(
        functools.partial(on_device, n=mesh.shape["elem"]), mesh=mesh,
        in_specs=in_specs, out_specs=out_specs, check_vma=False)
```
